128 devices in a mesh: sec: 4 (over x_lo, core), blk: 16 (over y, z), aux: 2 (over x_hi).
Axes of the slice: x: 4 (x_hi: 2, x_lo: 2; x = x_hi * 2 + x_lo), y: 4, z: 4, core: 2. Of those that a mesh axis runs over, the one named last changes fastest.
Arguments:
- half_ints: bfloat16 [16, 2048, 1024], P('blk', 'aux', 'sec'), may hold values from -0.59765625 to 0.59765625
- coeffs: bfloat16 [1024, 1024], replicated, may hold values from -0.1875 to 0.1875
- occ_energy: float32 [16], replicated, may hold values from -1.5 to -0.3
- vir_energy: float32 [1024], replicated, may hold values from 0.2 to 3
Outputs:
- back_density: float32 [1024, 16, 2048], P('sec', 'blk', 'aux')
The draws below stay inside these ranges and needn't reach their ends.
All inputs are finite; a program needn't handle non-finite values.
Results may differ from the reference program's by a relative error of at most 0.003.
Values may be sent and summed in bfloat16 or wider, within the bound.
No kernel may reach another device: no remote copies, remote signals or barrier semaphores. Data moves between devices by JAX's collectives and lax.ppermute only.
A program may use at most 64 MiB of HBM per device.

```python
import jax
import jax.numpy as jnp
from jax import lax

NOCC = 16
NVIR = 1024
NAUX = 2048
NBAS = 1024


def levels(own_key, dims, shards, least, largest):
    def one(position, parts):
        draws = jax.random.uniform(jax.random.fold_in(jax.random.fold_in(own_key, 6), position), (parts,), jnp.float32, least / len(shards), largest / len(shards))
        return jnp.repeat(jnp.exp(draws), dims[position] // parts).reshape((-1,) + (1,) * (len(dims) - position - 1))

    loudness = one(*shards[0])
    for cut in shards[1:]:
        loudness = loudness * one(*cut)
    return loudness


def gaussian(key, shape, width, limit, split=(), kind=jnp.bfloat16):
    loudness = levels(key, shape, split, -0.22, 0.18) if split else 1.0
    array = jax.random.normal(key, shape, jnp.float32) * width * loudness
    return jnp.minimum(jnp.maximum(array, -limit), limit).astype(kind)


def setup_inputs(seed: int = 0) -> dict:
    splits = jax.random.split(jax.random.key(seed), 5)
    return {
        "half_ints": gaussian(splits[0], (NOCC, NAUX, NBAS), 0.1, 0.59765625, ((0, 16), (1, 2), (2, 4))),
        "coeffs": gaussian(splits[1], (NBAS, NVIR), NBAS ** -0.5, 0.1875),
        "occ_energy": jnp.clip(jax.random.uniform(splits[2], (NOCC,), jnp.float32, -1.5, -0.3), -1.5, -0.3),
        "vir_energy": jnp.clip(jax.random.uniform(splits[3], (NVIR,), jnp.float32, 0.2, 3.0), 0.2, 3.0),
    }


def reference(half_ints, coeffs, occ_energy, vir_energy):
    high = lax.Precision.HIGHEST
    transformed = jnp.einsum("ipm,ma->ipa", half_ints.astype(jnp.float32), coeffs.astype(jnp.float32), precision=high).astype(jnp.bfloat16)
    trans_wide = lax.optimization_barrier(transformed).astype(jnp.float32)

    def per_occupied(index):
        own_rows = lax.dynamic_index_in_dim(trans_wide, index, 0, keepdims=False)
        tiles = jnp.einsum("pa,jpb->jab", own_rows, trans_wide, precision=high)
        own_energy = lax.dynamic_index_in_dim(occ_energy, index, 0, keepdims=False)
        denominator = own_energy + occ_energy[:, None, None] - vir_energy[None, :, None] - vir_energy[None, None, :]
        amplitude = (1.3 * tiles / denominator).astype(jnp.bfloat16)
        amplitude = lax.optimization_barrier(amplitude).astype(jnp.float32)
        return jnp.einsum("jab,jpb->pa", amplitude, trans_wide, precision=high)

    density = lax.map(per_occupied, jnp.arange(NOCC, dtype=jnp.int32))
    density_half = lax.optimization_barrier(density.astype(jnp.bfloat16)).astype(jnp.float32)
    return jnp.einsum("ma,ipa->mip", coeffs.astype(jnp.float32), density_half, precision=high)
```

```python
import itertools

import jax
import jax.numpy as jnp
import numpy as np
from jax import lax
from jax.sharding import PartitionSpec as P

AXES = ("sec", "blk", "aux")
BF, F32 = jnp.bfloat16, jnp.float32
Y1, Y2, Z1, Z2 = 4, 12, 1, 3
CHAINS = ((Y1, Y2, Z1, Z2), (Y2, Y1, Z2, Z1), (Z1, Z2, Y1, Y2), (Z2, Z1, Y2, Y1))


def flip(value, blk=0, chip=0, core=0):
    pairs = []
    for sec, b, aux in itertools.product(range(4), range(16), range(2)):
        x = (aux * 2 + sec // 2) ^ chip
        to = ((x % 2) * 2 + (sec % 2 ^ core)) * 32 + (b ^ blk) * 2 + x // 2
        pairs.append((sec * 32 + b * 2 + aux, to))
    return lax.ppermute(value, AXES, pairs)


def dot(left, right, dims):
    return lax.dot_general(left, right, (dims, ((), ())), preferred_element_type=F32)


def shards(half_ints, coeffs, occ_energy, vir_energy):
    sec, blk, aux = (lax.axis_index(name) for name in AXES)
    part = (aux * 2 + sec // 2) * 2 + sec % 2
    own = half_ints[0]
    near = flip(own, chip=1)
    far = flip(own, chip=2)
    side = flip(own, chip=3)
    own_c = flip(own, core=1)
    near_c = flip(near, core=1)
    far_c = flip(far, core=1)
    side_c = flip(side, core=1)
    slices = coeffs.reshape(4, 256, 1024)
    rel = jnp.concatenate([lax.dynamic_slice_in_dim(slices, sec ^ m, 1, 0)[0] for m in range(4)], 0)
    halves = [jnp.concatenate([own, own_c, near, near_c], 1), jnp.concatenate([far, far_c, side, side_c], 1)]
    cols = lax.dynamic_slice_in_dim(rel, part * 128, 128, 1)
    keys = jnp.concatenate([dot(cols, h, ((0,), (1,))).astype(BF) for h in halves], 1)
    query = jnp.concatenate([dot(rel, h, ((0,), (1,))).astype(BF) for h in halves], 1)

    four, third, last_a, last_b = [], [], [], []
    masks = [[], [], [], []]
    for k, (f1, f2, f3, f4) in enumerate(CHAINS):
        c1 = keys[32 * k : 32 * k + 32]
        c2 = jnp.concatenate([c1, flip(c1, blk=f1)], 0)
        c4 = jnp.concatenate([c2, flip(c2, blk=f2)], 0)
        r3 = flip(c4, blk=f3)
        four.append(c4)
        third.append(r3)
        last_a.append(flip(c4, blk=f4))
        last_b.append(flip(r3, blk=f4))
        base = [0, f1, f2, f1 ^ f2]
        for at, extra in enumerate((0, f3, f4, f3 ^ f4)):
            masks[at] += [m ^ extra for m in base]
    tokens = [jnp.concatenate(group, 0) for group in (four, third, last_a, last_b)]

    owner = blk ^ np.array(masks, np.int32).reshape(-1)
    occ_tok = jnp.sum(jnp.where(owner[:, None] == jnp.arange(16)[None], occ_energy[None], 0.0), 1)
    vir_tok = lax.dynamic_slice_in_dim(vir_energy, part * 128, 128).reshape(1, 4, 1, 32)
    token_level = (occ_tok.reshape(4, 4, 4, 1) - vir_tok).reshape(4, 512)
    own_occ = lax.dynamic_slice_in_dim(occ_energy, blk, 1)
    query_level = (own_occ - vir_energy)[:, None]

    amplitudes = []
    for at in range(4):
        tiles = dot(query, tokens[at], ((1,), (1,)))
        amplitudes.append((1.3 * tiles / (query_level + token_level[at][None])).astype(BF))
    amp = [jnp.concatenate(amplitudes[:2], 1), jnp.concatenate(amplitudes[2:], 1)]
    tok = [jnp.concatenate(tokens[:2], 0), jnp.concatenate(tokens[2:], 0)]
    density = dot(amp[0], tok[0], ((1,), (0,))) + dot(amp[1], tok[1], ((1,), (0,)))
    density = density.astype(BF)

    sums = []
    for half in (1, 0):
        back = dot(rel, density[:, 1024 * half : 1024 * half + 1024], ((1,), (0,)))
        give = back.reshape(4, 256, 1024)
        got = flip(jnp.concatenate([give[1], give[3]], 0).astype(BF), core=1)
        sums.append((give[0] + got[:256], give[2] + got[256:]))
    (far_sum, side_sum), (own_sum, near_sum) = sums
    total = own_sum + flip(near_sum.astype(BF), chip=1)
    total = total + flip(far_sum.astype(BF), chip=2) + flip(side_sum.astype(BF), chip=3)
    return total[:, None, :]


def solution(mesh):
    placed = (P("blk", "aux", "sec"), P(), P(), P())
    return jax.shard_map(
        shards, mesh=mesh, in_specs=placed, out_specs=P("sec", "blk", "aux"), check_vma=False
    )
```

```python
import itertools

import jax
import jax.numpy as jnp
import numpy as np
from jax import lax
from jax.sharding import PartitionSpec as P

AXES = ("sec", "blk", "aux")
BF, F32 = jnp.bfloat16, jnp.float32
Y1, Y2, Z1, Z2 = 4, 12, 1, 3
CHAINS = (
    ((Y1, Z1), (Y2, Z2), (Z1, Y1), (Z2, Y2)),
    ((Y2, Z2), (Y1, Z1), (Z2, Y2), (Z1, Y1)),
)


def flip(value, blk=(0, 0), chip=0, core=0):
    pairs = []
    for sec, b, aux in itertools.product(range(4), range(16), range(2)):
        x = (aux * 2 + sec // 2) ^ chip
        to = ((x % 2) * 2 + (sec % 2 ^ core)) * 32 + (b ^ blk[sec % 2]) * 2 + x // 2
        pairs.append((sec * 32 + b * 2 + aux, to))
    return lax.ppermute(value, AXES, pairs)


def _dot(left, right, dims):
    return lax.dot_general(left, right, (dims, ((), ())), preferred_element_type=F32)


def cat(parts, axis=0):
    return jnp.concatenate(parts, axis)


def work(half_ints, coeffs, occ_energy, vir_energy):
    sec, blk, aux = (lax.axis_index(name) for name in AXES)
    core = sec % 2
    part = (aux * 2 + sec // 2) * 2 + core
    own = half_ints[0]
    near = flip(own, chip=1)
    side = flip(own, chip=3)
    far = flip(own, chip=2)
    own_c = flip(own, core=1)
    near_c = flip(near, core=1)
    side_c = flip(side, core=1)
    far_c = flip(far, core=1)
    slices = coeffs.reshape(4, 256, 1024)
    rel = cat([lax.dynamic_slice_in_dim(slices, sec ^ m, 1, 0)[0] for m in range(4)])
    cols = lax.dynamic_slice_in_dim(rel, part * 128, 128, 1)

    query, batches, masks = [], [[], [], [], []], [[], [], [], []]
    for pieces in ((own, own_c, near, near_c), (far, far_c, side, side_c)):
        block = cat(lax.optimization_barrier(pieces), 1)
        keys = _dot(cols, block, ((0,), (1,))).astype(BF)
        query.append(_dot(rel, block, ((0,), (1,))).astype(BF))
        groups = [[], [], [], []]
        starts = lax.optimization_barrier((keys[:64], keys[64:]))
        for c1, (f1, f2, f3, f4) in zip(starts, CHAINS):
            c2 = cat([c1, flip(c1, blk=f1)])
            c4 = cat([c2, flip(c2, blk=f2)])
            r3 = flip(c4, blk=f3)
            r4 = flip(c4, blk=f4)
            r5 = flip(r3, blk=f4)
            for group, value in zip(groups, (c4, r3, r4, r5)):
                group.append(value)
        for batch, group in zip(batches, groups):
            batch.append(cat(group))
    for f1, f2, f3, f4 in (np.array(chain) for chain in CHAINS):
        for at, extra in enumerate((0 * f1, f3, f4, f3 ^ f4)):
            masks[at] += [m ^ extra for m in (0 * f1, f1, f2, f1 ^ f2)]

    masks = np.array(masks, np.int32).reshape(32, 2)
    owner = blk ^ jnp.where(core == 0, masks[:, 0], masks[:, 1])
    occ_tok = jnp.sum(jnp.where(owner[:, None] == jnp.arange(16)[None], occ_energy[None], 0.0), 1)
    vir_tok = lax.dynamic_slice_in_dim(vir_energy, part * 128, 128).reshape(1, 2, 1, 64)
    key_level = (occ_tok.reshape(4, 2, 4, 1) - vir_tok).reshape(4, 512)
    own_occ = lax.dynamic_slice_in_dim(occ_energy, blk, 1)
    query_level = (own_occ - vir_energy)[:, None]

    query = cat(query, 1)
    turned = []
    for at, pair in enumerate(batches):
        tiles = _dot(query, cat(pair, 1), ((1,), (1,)))
        amplitude = (1.3 * tiles / (query_level + key_level[at][None])).astype(BF)
        amplitude = lax.optimization_barrier(amplitude)
        turned.append(_dot(rel, amplitude, ((1,), (0,))).astype(BF))
    turned = cat(turned, 1)
    values = [cat([pair[h] for pair in batches]) for h in range(2)]

    def back(rows, h):
        return _dot(cat([turned[256 * r : 256 * r + 256] for r in rows]), values[h], ((1,), (0,)))

    given = [flip(back((1, 3), h).astype(BF), core=1) for h in range(2)]
    far_sum, side_sum = jnp.split(lax.optimization_barrier(back((0, 2), 1)) + given[1], 2)
    own_sum, near_sum = jnp.split(lax.optimization_barrier(back((0, 2), 0)) + given[0], 2)
    far_got = flip(far_sum.astype(BF), chip=2)
    side_got = flip(side_sum.astype(BF), chip=3)
    near_got = flip(near_sum.astype(BF), chip=1)
    return (own_sum + far_got + side_got + near_got)[:, None, :]


def solution(mesh):
    placed = (P("blk", "aux", "sec"), P(), P(), P())
    return jax.shard_map(work, mesh=mesh, in_specs=placed, out_specs=P("sec", "blk", "aux"), check_vma=False)
```

```python
import functools
import itertools

import jax
import jax.numpy as jnp
import numpy as np
from jax import lax
from jax.experimental import pallas as pl
from jax.experimental.pallas import tpu as pltpu
from jax.sharding import PartitionSpec as P

AXES = ("sec", "blk", "aux")
BF, F32 = jnp.bfloat16, jnp.float32
Y1, Y2, Z1, Z2 = 4, 12, 1, 3
CHAINS = (
    ((Y1, Z1), (Y2, Z2), (Z1, Y1), (Z2, Y2)),
    ((Y2, Z2), (Y1, Z1), (Z2, Y2), (Z1, Y1)),
)


def flip(value, blk=(0, 0), chip=(0, 0), core=0):
    pairs = []
    for sec, b, aux in itertools.product(range(4), range(16), range(2)):
        x = (aux * 2 + sec // 2) ^ chip[sec % 2]
        to = ((x % 2) * 2 + (sec % 2 ^ core)) * 32 + (b ^ blk[sec % 2]) * 2 + x // 2
        pairs.append((sec * 32 + b * 2 + aux, to))
    return lax.ppermute(value, AXES, pairs)


def _dot(left, right, dims):
    return lax.dot_general(left, right, (dims, ((), ())), preferred_element_type=F32)


def cat(parts, axis=0):
    return jnp.concatenate(parts, axis)


def half_kernel(q0, first, second, out):
    @pl.loop(0, 4)
    def _(i):
        rows = pl.ds(pl.multiple_of(i * 256, 256), 256)
        out[rows, :256] = _dot(q0[rows, :], first[...], ((1,), (1,)))
        out[rows, 256:] = _dot(q0[rows, :], second[...], ((1,), (1,)))


def mix_kernel(at, q1, tiles, first, second, rel, q_level, k_level, *refs):
    out, amp = refs[-2:]

    @pl.loop(0, 4)
    def _(i):
        rows = pl.ds(pl.multiple_of(i * 256, 256), 256)
        for k, keys in enumerate((first, second)):
            cols = slice(256 * k, 256 * k + 256)
            total = tiles[rows, cols] + _dot(q1[rows, :], keys[...], ((1,), (1,)))
            amp[rows, cols] = (1.3 * total / (q_level[rows, :] + k_level[:, cols])).astype(BF)

    @pl.loop(0, 4)
    def _(i):
        rows = pl.ds(pl.multiple_of(i * 256, 256), 256)
        out[rows, 512 * at : 512 * at + 512] = _dot(rel[rows, :], amp[...], ((1,), (0,))).astype(BF)


def finish_kernel(own, first, second, out):
    for j in range(8):
        cols = slice(128 * j, 128 * j + 128)
        out[:, j, :] = own[:, cols] + first[:, cols].astype(F32) + second[:, cols].astype(F32)


def kernel(body, args, shape, dtype, scratch=(), aliases=None, flops=0, limit=12 << 20):
    spec = pl.BlockSpec(memory_space=pltpu.VMEM)
    return pl.pallas_call(
        body,
        out_shape=jax.ShapeDtypeStruct(shape, dtype),
        in_specs=[spec] * len(args),
        out_specs=spec,
        scratch_shapes=scratch,
        input_output_aliases=aliases or {},
        compiler_params=pltpu.CompilerParams(vmem_limit_bytes=limit),
        cost_estimate=pl.CostEstimate(flops=flops, bytes_accessed=2**21, transcendentals=0),
    )(*args)


def work(half_ints, coeffs, occ_energy, vir_energy):
    sec, blk, aux = (lax.axis_index(name) for name in AXES)
    core = sec % 2
    part = (aux * 2 + sec // 2) * 2 + core
    own = half_ints[0]
    near = flip(own, chip=(1, 1))
    side = flip(own, chip=(3, 3))
    far = flip(own, chip=(2, 2))
    own_c = flip(own, core=1)
    near_c = flip(near, core=1)
    side_c = flip(side, core=1)
    far_c = flip(far, core=1)
    slices = coeffs.reshape(4, 256, 1024)
    rel = cat([lax.dynamic_slice_in_dim(slices, sec ^ m, 1, 0)[0] for m in range(4)])
    cols = lax.dynamic_slice_in_dim(rel, part * 128, 128, 1)

    query, batches, masks = [], [[], [], [], []], [[], [], [], []]
    for pieces in ((own, own_c, near, near_c), (far, far_c, side, side_c)):
        block = cat(lax.optimization_barrier(pieces), 1)
        keys = _dot(cols, block, ((0,), (1,))).astype(BF)
        query.append(_dot(rel, block, ((0,), (1,))).astype(BF))
        groups = [[], [], [], []]
        starts = lax.optimization_barrier((keys[:64], keys[64:]))
        for c1, (f1, f2, f3, f4) in zip(starts, CHAINS):
            c2 = cat([c1, flip(c1, blk=f1)])
            c4 = cat([c2, flip(c2, blk=f2)])
            r3 = flip(c4, blk=f3)
            r4 = flip(c4, blk=f4)
            r5 = flip(r3, blk=f4)
            for group, value in zip(groups, (c4, r3, r4, r5)):
                group.append(value)
        for batch, group in zip(batches, groups):
            batch.append(group)
    for f1, f2, f3, f4 in (np.array(chain) for chain in CHAINS):
        for at, extra in enumerate((0 * f1, f3, f4, f3 ^ f4)):
            masks[at] += [m ^ extra for m in (0 * f1, f1, f2, f1 ^ f2)]

    masks = np.array(masks, np.int32).reshape(32, 2)
    owner = blk ^ jnp.where(core == 0, masks[:, 0], masks[:, 1])
    occ_tok = jnp.sum(jnp.where(owner[:, None] == jnp.arange(16)[None], occ_energy[None], 0.0), 1)
    vir_tok = lax.dynamic_slice_in_dim(vir_energy, part * 128, 128).reshape(1, 2, 1, 64)
    key_level = (occ_tok.reshape(4, 2, 4, 1) - vir_tok).reshape(4, 512)
    own_occ = lax.dynamic_slice_in_dim(occ_energy, blk, 1)
    query_level = (own_occ - vir_energy)[:, None]

    turned = None
    for at, (first, second) in enumerate(batches):
        tiles = kernel(half_kernel, [query[0], *first], (1024, 512), F32, flops=2**30)
        args = [query[1], tiles, *second, rel, query_level, key_level[at][None]]
        aliases = None if at == 0 else {len(args): 0}
        args += [] if at == 0 else [turned]
        turned = kernel(
            functools.partial(mix_kernel, at), args, (1024, 2048), BF,
            scratch=[pltpu.VMEM((1024, 512), BF)], aliases=aliases, flops=2**31,
        )
    values = [cat([piece for pair in batches for piece in pair[h]]) for h in range(2)]

    def back(rows, h):
        both = _dot(turned[512 * rows : 512 * rows + 512], values[h], ((1,), (0,)))
        keep, give = lax.optimization_barrier((both[:256], both[256:].astype(BF)))
        return keep + flip(give, core=1)

    far_sum = back(0, 1)
    side_sum = back(1, 1)
    near_sum = back(1, 0)
    own_sum = back(0, 0)
    via = flip(far_sum.astype(BF), chip=(3, 1))
    message, rest = lax.optimization_barrier(
        (jnp.where(core == 0, side_sum, near_sum).astype(BF), jnp.where(core == 0, near_sum, side_sum))
    )
    direct = flip(message, chip=(3, 1))
    last = flip((rest + via).astype(BF), chip=(1, 3))
    total = kernel(finish_kernel, [own_sum, direct, last], (256, 8, 128), F32)
    return total.reshape(256, 1, 1024)


def solution(mesh):
    placed = (P("blk", "aux", "sec"), P(), P(), P())
    return jax.shard_map(work, mesh=mesh, in_specs=placed, out_specs=P("sec", "blk", "aux"), check_vma=False)
```
